32 devices in a mesh: groups: 2 (over x), grid: 8 (over z, y), dp: 2 (over core).
Axes of the slice: x: 2, y: 2, z: 4, core: 2. Of those that a mesh axis runs over, the one named last changes fastest.
Arguments:
- rot_grads: bfloat16 [4096, 4096], P('grid', ('groups', 'dp')), parts along dimension 1, may hold values from -1 to 1
- rot_inputs: bfloat16 [28672, 4096], P('grid', ('groups', 'dp')), parts along dimension 1, may hold values from -6 to 6
- lengths: int32 [16], P(('groups', 'dp')), parts along dimension 0, may hold values from 1 to 256, as said below
- token_mask: int32 [4096], P(('groups', 'dp')), parts along dimension 0, may hold values 0 or 1
Outputs:
- correction: float32 [57344, 4096], P(('groups', 'grid'), 'dp'), parts along dimension 0
The draws below stay inside these ranges and needn't reach their ends.
There are 2 independent parts, one for each index of `groups`. The reference program is written for one: setup_inputs(seed, part) draws one part's arguments, and reference() takes and returns one part's arrays. A program takes and returns all parts, laid end to end along the dimension named above; each array names one. Nothing has to cross between parts.
Inputs may be any that keep to these rules, and one draw needn't show every extreme that they name: `lengths`: each span holds at least one sequence token, and at least one span is full (256 tokens).
All inputs are finite; a program needn't handle non-finite values. No bound on the sum of `token_mask` on one device may be relied on, other than what follows from the above.
Results may differ from the reference program's by a relative error of at most 0.0003.
Values may be sent and summed in bfloat16 or wider, within the bound.
A program may use at most 448 MiB of HBM per device.

```python
import jax
import jax.numpy as jnp

O = 4096
I = 28672
LEN = 256
SPANS = 8
TOKENS = 2048


def draw_lengths(key, part):
    first_key = jax.random.fold_in(key, 11)
    second_key = jax.random.fold_in(key, 23)
    base_lengths = jax.random.randint(first_key, (SPANS,), LEN // 4, LEN + 1)
    chosen = jax.random.randint(second_key, (), 0, SPANS)
    filled = jnp.where(jnp.arange(SPANS) == chosen, LEN, base_lengths)
    return filled.astype(jnp.int32)


def touch_ends(drawn, key, smallest, top_value):
    index_at = [jax.random.randint(jax.random.fold_in(key, axis), (), 0, length) for axis, length in enumerate(drawn.shape)]
    longest = drawn.shape.index(max(drawn.shape))
    next_to = index_at[:longest] + [(index_at[longest] + 1) % drawn.shape[longest]] + index_at[longest + 1:]
    return drawn.at[tuple(index_at)].set(smallest).at[tuple(next_to)].set(top_value)


def level_of(rng, shape, pieces, smallest, top_value):
    loudness = 1.0
    for axis_at, shards_of in pieces:
        heights = jax.random.uniform(jax.random.fold_in(jax.random.fold_in(rng, 6), axis_at), (shards_of,), jnp.float32, smallest / len(pieces), top_value / len(pieces))
        loudness = loudness * jnp.repeat(jnp.exp(heights), shape[axis_at] // shards_of).reshape((-1,) + (1,) * (len(shape) - 1 - axis_at))
    return loudness


def bell_draw(stream_key, dims, deviation, limit, shards=(), kind=jnp.bfloat16):
    array = jax.random.normal(stream_key, dims, jnp.float32) * deviation
    if len(shards) > 0:
        array = level_of(stream_key, dims, shards, -0.22, 0.18) * array
    return jnp.clip(array, min=-limit, max=limit).astype(kind)


def setup_inputs(seed: int = 0, part: int = 0) -> dict:
    seeds = jax.random.split(jax.random.key(seed), 5)
    part_splits = jax.random.split(jax.random.fold_in(seeds[4], part), 5)
    return {
        "rot_grads": bell_draw(part_splits[0], (O, TOKENS), (LEN ** -0.5), 1.0, ((0, 8), (1, 2))),
        "rot_inputs": bell_draw(part_splits[1], (I, TOKENS), 1.0, 6.0, ((0, 8), (1, 2))),
        "lengths": draw_lengths(jax.random.fold_in(jax.random.fold_in(seeds[4], part), 71), part),
        "token_mask": touch_ends((jax.random.randint(part_splits[3], (TOKENS,), 0, 4) < 3).astype(jnp.int32), jax.random.fold_in(part_splits[3], 1), 0, 1),
    }


def reference(rot_grads, rot_inputs, lengths, token_mask):
    slot_ids = jnp.arange(LEN, dtype=jnp.int32)
    inside = (slot_ids[None, :] < lengths[:, None]).astype(jnp.int32).reshape(-1)
    usable = token_mask * inside
    weighted = rot_inputs * usable.astype(jnp.bfloat16)[None, :]
    running = jnp.zeros((I, O), jnp.float32)
    for span_id in range(SPANS):
        left_block = weighted[:, span_id * LEN:(span_id + 1) * LEN].astype(jnp.float32)
        right_block = rot_grads[:, span_id * LEN:(span_id + 1) * LEN].astype(jnp.float32)
        products = jnp.dot(left_block, right_block.T, preferred_element_type=jnp.float32)
        running = running + products * products
    return running / SPANS
```

```python
import functools

import jax
import jax.numpy as jnp
from jax import lax
from jax.experimental import pallas as pl
from jax.experimental.pallas import tpu as pltpu
from jax.sharding import PartitionSpec as P

LEN = 256
CHUNKS = 2
MESH = pl.DeviceIdType.MESH


def grid_sides(grid_size):
    inner = 1
    while (inner * 2) * (inner * 2) <= grid_size:
        inner *= 2
    return grid_size // inner, inner


def gather_kernel(nz, ny, chunks, g_ref, x_ref, gbuf, xbuf, own_send, fwd_send, recv, local_sem, x_sems):
    grid = lax.axis_index("grid")
    core = lax.axis_index("dp")
    z = grid // ny
    y = grid % ny
    zh = nz // 2
    half = zh * ny
    rows = g_ref.shape[0] // chunks

    up, down = z < nz - 1, z > 0
    right, left = y < ny - 1, y > 0
    barrier = pltpu.get_barrier_semaphore()
    for there, target in ((up, grid + ny), (down, grid - ny), (right, grid + 1), (left, grid - 1)):
        @pl.when(there)
        def _():
            for other in range(2):
                pl.semaphore_signal(
                    barrier, inc=1, device_id={"grid": target, "dp": other}, device_id_type=MESH
                )
    pl.semaphore_signal(barrier, inc=1, device_id={"dp": 1 - core}, device_id_type=MESH)
    neighbours = sum(there.astype(jnp.int32) for there in (up, down, right, left))
    pl.semaphore_wait(barrier, 2 * neighbours + 1)

    def piece(slot, index, c):
        return gbuf.at[slot, index, pl.ds(pl.multiple_of(c * rows, rows), rows)]

    def send(src, slot, index, c, sem, target, target_core):
        return pltpu.make_async_remote_copy(
            src_ref=src,
            dst_ref=piece(slot, index, c),
            send_sem=sem,
            recv_sem=recv.at[slot, index, c],
            device_id={"grid": target, "dp": target_core},
            device_id_type=MESH,
        )

    owner = z // zh
    own_slot = jnp.where(core == owner, 0, 1)
    own_index = grid - owner * half

    def own_copies(c):
        src = g_ref.at[pl.ds(pl.multiple_of(c * rows, rows), rows)]
        return [
            (there, send(src, own_slot, own_index, c, own_send.at[c, k], target, owner))
            for k, (there, target) in enumerate(
                ((up, grid + ny), (down, grid - ny), (right, grid + 1), (left, grid - 1), (core != owner, grid))
            )
        ]

    local = pltpu.make_async_copy(g_ref, gbuf.at[0, own_index], local_sem)

    @pl.loop(0, chunks)
    def _(c):
        for there, copy in own_copies(c):
            @pl.when(there)
            def _():
                copy.start()

    x_copy = pltpu.make_async_remote_copy(
        src_ref=x_ref, dst_ref=xbuf, send_sem=x_sems.at[0], recv_sem=x_sems.at[1],
        device_id={"dp": 1 - core}, device_id_type=MESH,
    )
    x_copy.start()

    @pl.when(core == owner)
    def _():
        local.start()

    def column_copies(step, sign, q):
        c, slot = q // 2, q % 2
        index = (z - sign * step) * ny + y - core * half
        src = piece(slot, index, c)
        onward = z + sign
        return [
            (there, send(src, slot, index, c, fwd_send.at[slot, index, c, k], target, core))
            for k, (there, target) in enumerate(
                (((onward >= 0) & (onward < nz), grid + sign * ny), (right, grid + 1), (left, grid - 1))
            )
        ]

    def row_copies(step, sign, q):
        j, c, slot = q // (2 * chunks), (q // 2) % chunks, q % 2
        zi = jnp.where(z <= core * zh, j, zh - 1 - j)
        index = zi * ny + y - sign * step
        onward = y + sign
        return [
            ((onward >= 0) & (onward < ny), send(
                piece(slot, index, c), slot, index, c, fwd_send.at[slot, index, c, 0], grid + sign, core))
        ]

    def walk(act):
        for step in range(1, nz):
            for sign in (1, -1):
                source = z - sign * step

                @pl.when((source >= core * zh) & (source < core * zh + zh))
                def _():
                    @pl.loop(0, 2 * chunks)
                    def _(q):
                        act(column_copies(step, sign, q))
        for step in range(1, ny):
            for sign in (1, -1):
                source = y - sign * step

                @pl.when((source >= 0) & (source < ny))
                def _():
                    @pl.loop(0, zh * 2 * chunks)
                    def _(q):
                        act(row_copies(step, sign, q))

    def forward(copies):
        copies[0][1].wait_recv()
        for there, copy in copies:
            @pl.when(there)
            def _():
                copy.start()

    def finish(copies):
        for there, copy in copies:
            @pl.when(there)
            def _():
                copy.wait_send()

    walk(forward)

    @pl.when(core == owner)
    def _():
        @pl.loop(0, chunks)
        def _(c):
            send(piece(1, own_index, c), 1, own_index, c, own_send.at[c, 4], grid, 1 - core).wait_recv()
        local.wait()

    @pl.loop(0, chunks)
    def _(c):
        finish(own_copies(c))

    walk(finish)
    x_copy.wait()


def square_kernel(scale, g_ref, own_ref, peer_ref, out_ref):
    width = 256
    for at in range(0, out_ref.shape[1], width):
        total = None
        for which, x_ref in enumerate((own_ref, peer_ref)):
            for start in range(0, x_ref.shape[1], LEN):
                product = lax.dot_general(
                    x_ref[:, start:start + LEN],
                    g_ref[which, at:at + width, start:start + LEN],
                    (((1,), (1,)), ((), ())),
                    preferred_element_type=jnp.float32,
                )
                square = product * product
                total = square if total is None else total + square
        out_ref[:, at:at + width] = total * scale


def per_device(rot_grads, rot_inputs, lengths, token_mask):
    nz, ny = grid_sides(lax.axis_size("grid"))
    rows, tokens = rot_grads.shape
    features = rot_inputs.shape[0]
    half = nz * ny // 2
    chunks = CHUNKS if rows % (CHUNKS * 128) == 0 else 1
    slot_ids = jnp.arange(LEN, dtype=jnp.int32)
    inside = (slot_ids[None, :] < lengths[:, None]).astype(jnp.int32).reshape(-1)
    usable = token_mask * inside
    weighted = rot_grads * usable.astype(jnp.bfloat16)[None, :]

    dma = pltpu.SemaphoreType.DMA
    gathered, peer_inputs = pl.pallas_call(
        functools.partial(gather_kernel, nz, ny, chunks),
        out_shape=(
            jax.ShapeDtypeStruct((2, half, rows, tokens), jnp.bfloat16),
            jax.ShapeDtypeStruct((features, tokens), jnp.bfloat16),
        ),
        in_specs=[pl.BlockSpec(memory_space=pl.ANY)] * 2,
        out_specs=[pl.BlockSpec(memory_space=pl.ANY)] * 2,
        scratch_shapes=[
            dma((chunks, 5)),
            dma((2, half, chunks, 3)),
            dma((2, half, chunks)),
            dma,
            dma((2,)),
        ],
        compiler_params=pltpu.CompilerParams(collective_id=0, has_side_effects=True),
        name="gather",
    )(weighted, rot_inputs)

    columns = half * rows
    gathered = gathered.reshape(2, columns, tokens)
    tile = next(t for t in (512, 448, 256, 64, 8) if features % t == 0)
    spans = lengths.shape[0] * lax.axis_size("dp")
    return pl.pallas_call(
        functools.partial(square_kernel, 1.0 / spans),
        grid=(features // tile,),
        out_shape=jax.ShapeDtypeStruct((features, columns), jnp.float32),
        in_specs=[
            pl.BlockSpec((2, columns, tokens), lambda i: (0, 0, 0), pipeline_mode=pl.Buffered(1)),
            pl.BlockSpec((tile, tokens), lambda i: (i, 0)),
            pl.BlockSpec((tile, tokens), lambda i: (i, 0)),
        ],
        out_specs=pl.BlockSpec((tile, columns), lambda i: (i, 0)),
        compiler_params=pltpu.CompilerParams(vmem_limit_bytes=48 * 2**20),
        name="squares",
    )(gathered, rot_inputs, peer_inputs)


def solution(mesh):
    return jax.shard_map(
        per_device,
        mesh=mesh,
        in_specs=(
            P("grid", ("groups", "dp")),
            P("grid", ("groups", "dp")),
            P(("groups", "dp")),
            P(("groups", "dp")),
        ),
        out_specs=P(("groups", "grid"), "dp"),
        check_vma=False,
    )
```

```python
import functools

import jax
import jax.numpy as jnp
from jax import lax
from jax.experimental import pallas as pl
from jax.experimental.pallas import tpu as pltpu
from jax.sharding import PartitionSpec as P

LEN = 256
CHUNKS = 2
TAIL_TILE = 256
GRANT = 18 * 2**20
MESH = pl.DeviceIdType.MESH


def grid_sides(grid_size):
    inner = 1
    while (inner * 2) * (inner * 2) <= grid_size:
        inner *= 2
    return grid_size // inner, inner


def gather_kernel(nz, ny, chunks, g_ref, x_ref, gbuf, xbuf, own_send, fwd_send, recv, local_sem, x_sems):
    grid = lax.axis_index("grid")
    core = lax.axis_index("dp")
    z = grid // ny
    y = grid % ny
    zh = nz // 2
    half = zh * ny
    rows = g_ref.shape[0] // chunks

    up, down = z < nz - 1, z > 0
    right, left = y < ny - 1, y > 0
    barrier = pltpu.get_barrier_semaphore()
    for there, target in ((up, grid + ny), (down, grid - ny), (right, grid + 1), (left, grid - 1)):
        @pl.when(there)
        def _():
            for other in range(2):
                pl.semaphore_signal(
                    barrier, inc=1, device_id={"grid": target, "dp": other}, device_id_type=MESH
                )
    pl.semaphore_signal(barrier, inc=1, device_id={"dp": 1 - core}, device_id_type=MESH)
    neighbours = sum(there.astype(jnp.int32) for there in (up, down, right, left))
    pl.semaphore_wait(barrier, 2 * neighbours + 1)

    def piece(slot, index, c):
        return gbuf.at[slot, index, pl.ds(pl.multiple_of(c * rows, rows), rows)]

    def send(src, slot, index, c, sem, target, target_core):
        return pltpu.make_async_remote_copy(
            src_ref=src,
            dst_ref=piece(slot, index, c),
            send_sem=sem,
            recv_sem=recv.at[slot, index, c],
            device_id={"grid": target, "dp": target_core},
            device_id_type=MESH,
        )

    owner = z // zh
    own_slot = jnp.where(core == owner, 0, 1)
    own_index = grid - owner * half

    def own_copies(c):
        src = g_ref.at[pl.ds(pl.multiple_of(c * rows, rows), rows)]
        return [
            (there, send(src, own_slot, own_index, c, own_send.at[c, k], target, owner))
            for k, (there, target) in enumerate(
                ((up, grid + ny), (down, grid - ny), (right, grid + 1), (left, grid - 1), (core != owner, grid))
            )
        ]

    local = pltpu.make_async_copy(g_ref, gbuf.at[0, own_index], local_sem)

    @pl.loop(0, chunks)
    def _(c):
        for there, copy in own_copies(c):
            @pl.when(there)
            def _():
                copy.start()

    x_copy = pltpu.make_async_remote_copy(
        src_ref=x_ref, dst_ref=xbuf, send_sem=x_sems.at[0], recv_sem=x_sems.at[1],
        device_id={"dp": 1 - core}, device_id_type=MESH,
    )
    x_copy.start()

    @pl.when(core == owner)
    def _():
        local.start()

    def column_copies(step, sign, q):
        c, slot = q // 2, q % 2
        index = (z - sign * step) * ny + y - core * half
        src = piece(slot, index, c)
        onward = z + sign
        return [
            (there, send(src, slot, index, c, fwd_send.at[slot, index, c, k], target, core))
            for k, (there, target) in enumerate(
                (((onward >= 0) & (onward < nz), grid + sign * ny), (right, grid + 1), (left, grid - 1))
            )
        ]

    def row_copies(step, sign, q):
        j, c, slot = q // (2 * chunks), (q // 2) % chunks, q % 2
        zi = jnp.where(z <= core * zh, j, zh - 1 - j)
        index = zi * ny + y - sign * step
        onward = y + sign
        return [
            ((onward >= 0) & (onward < ny), send(
                piece(slot, index, c), slot, index, c, fwd_send.at[slot, index, c, 0], grid + sign, core))
        ]

    def walk(act):
        for step in range(1, nz):
            for sign in (1, -1):
                source = z - sign * step

                @pl.when((source >= core * zh) & (source < core * zh + zh))
                def _():
                    @pl.loop(0, 2 * chunks)
                    def _(q):
                        act(column_copies(step, sign, q))
        for step in range(1, ny):
            for sign in (1, -1):
                source = y - sign * step

                @pl.when((source >= 0) & (source < ny))
                def _():
                    @pl.loop(0, zh * 2 * chunks)
                    def _(q):
                        act(row_copies(step, sign, q))

    def forward(copies):
        copies[0][1].wait_recv()
        for there, copy in copies:
            @pl.when(there)
            def _():
                copy.start()

    def finish(copies):
        for there, copy in copies:
            @pl.when(there)
            def _():
                copy.wait_send()

    walk(forward)

    @pl.when(core == owner)
    def _():
        @pl.loop(0, chunks)
        def _(c):
            send(piece(1, own_index, c), 1, own_index, c, own_send.at[c, 4], grid, 1 - core).wait_recv()
        local.wait()

    @pl.loop(0, chunks)
    def _(c):
        finish(own_copies(c))

    walk(finish)
    x_copy.wait()


def square_kernel(scale, g_ref, own_ref, peer_ref, out_ref):
    width = 256
    for at in range(0, out_ref.shape[1], width):
        total = None
        for which, x_ref in enumerate((own_ref, peer_ref)):
            for start in range(0, x_ref.shape[1], LEN):
                product = lax.dot_general(
                    x_ref[:, start:start + LEN],
                    g_ref[which, at:at + width, start:start + LEN],
                    (((1,), (1,)), ((), ())),
                    preferred_element_type=jnp.float32,
                )
                square = product * product
                total = square if total is None else total + square
        out_ref[:, at:at + width] = total * scale


def pieces_of(rows):
    if rows % 512:
        return ((0, rows, False),)
    unit = rows // 512
    cuts = (0, 32, 128, 256, 384, 512)
    return tuple((a * unit, (b - a) * unit, a == 0) for a, b in zip(cuts, cuts[1:]))


def squares(scale, tokens, x_of, g_of):
    total = None
    for which in range(2):
        for start in range(0, tokens, LEN):
            product = lax.dot_general(
                x_of(which, start),
                g_of(which, start),
                (((1,), (1,)), ((), ())),
                preferred_element_type=jnp.float32,
            )
            square = product * product
            total = square if total is None else total + square
    return total * scale


def gather_squares_kernel(
    nz, tile, scale, g_ref, mask_ref, lengths_ref, x_ref, gbuf, xbuf, done_ref,
    masked, held, x_tiles, outs, own_send, fwd_send, recv, local_sem, x_sems, held_sems, tile_sems, peer_sems, out_sems,
):
    ny = 2
    grid = lax.axis_index("grid")
    core = lax.axis_index("dp")
    z = grid // ny
    y = grid % ny
    zh = nz // 2
    half = zh * ny
    rows, tokens = g_ref.shape
    pieces = pieces_of(rows)
    across = grid + 1 - 2 * y

    up, down = z < nz - 1, z > 0
    barrier = pltpu.get_barrier_semaphore()
    for other in range(2):
        @pl.when(up)
        def _():
            pl.semaphore_signal(barrier, inc=1, device_id={"grid": grid + ny, "dp": other}, device_id_type=MESH)

        @pl.when(down)
        def _():
            pl.semaphore_signal(barrier, inc=1, device_id={"grid": grid - ny, "dp": other}, device_id_type=MESH)

        pl.semaphore_signal(barrier, inc=1, device_id={"grid": across, "dp": other}, device_id_type=MESH)
    pl.semaphore_signal(barrier, inc=1, device_id={"dp": 1 - core}, device_id_type=MESH)

    for start in range(0, tokens, LEN):
        slot_ids = lax.broadcasted_iota(jnp.int32, (1, LEN), 1)
        usable = jnp.where(slot_ids < lengths_ref[start // LEN], mask_ref[:, start:start + LEN], 0)
        weights = usable.astype(jnp.float32).astype(jnp.bfloat16)
        masked[:, start:start + LEN] = g_ref[:, start:start + LEN] * weights

    pl.semaphore_wait(barrier, 2 * (up.astype(jnp.int32) + down.astype(jnp.int32)) + 3)

    def part(slot, index, c):
        return gbuf.at[slot, index, pl.ds(pieces[c][0], pieces[c][1])]

    def send(src, slot, index, c, sem, target, target_core):
        return pltpu.make_async_remote_copy(
            src_ref=src,
            dst_ref=part(slot, index, c),
            send_sem=sem,
            recv_sem=recv.at[slot, index, c],
            device_id={"grid": target, "dp": target_core},
            device_id_type=MESH,
        )

    owner = z // zh
    own_slot = jnp.where(core == owner, 0, 1)
    own_index = grid - owner * half

    def own_copies(c):
        src = masked.at[pl.ds(pieces[c][0], pieces[c][1])]
        return [
            (there, send(src, own_slot, own_index, c, own_send.at[c, k], target, owner))
            for k, (there, target) in enumerate(
                ((None, across), (up, grid + ny), (down, grid - ny), (core != owner, grid))
            )
        ]

    def each(copies, act):
        for there, copy in copies:
            if there is None:
                act(copy)
            else:
                pl.when(there)(functools.partial(act, copy))

    for c in range(len(pieces)):
        each(own_copies(c), lambda copy: copy.start())

    x_copy = pltpu.make_async_remote_copy(
        src_ref=x_ref, dst_ref=xbuf, send_sem=x_sems.at[0], recv_sem=x_sems.at[1],
        device_id={"dp": 1 - core}, device_id_type=MESH,
    )
    x_copy.start()
    local = pltpu.make_async_copy(masked, held.at[0], local_sem)

    @pl.when(core == owner)
    def _():
        local.start()

    def onward(slot, index, c, source, own_column):
        src = part(slot, index, c)
        y_first = pieces[c][2]
        if own_column or y_first:
            yield up & (z >= source), send(src, slot, index, c, fwd_send.at[slot, index, c, 0], grid + ny, core)
            yield down & (z <= source), send(src, slot, index, c, fwd_send.at[slot, index, c, 1], grid - ny, core)
        if own_column and not y_first:
            yield None, send(src, slot, index, c, fwd_send.at[slot, index, c, 2], across, core)

    def arrived(slot, index, c):
        send(part(slot, index, c), slot, index, c, fwd_send.at[slot, index, c, 2], across, core).wait_recv()

    near = jnp.where(z <= core * zh, 0, 1)
    far = 1 - near

    def group(zi, c, own_column, wait_first, act):
        source = core * zh + zi
        index = zi * ny + (y if own_column else 1 - y)

        def step():
            @pl.loop(0, 2)
            def _(slot):
                if wait_first:
                    arrived(slot, index, c)
                each(onward(slot, index, c, source, own_column), act)

        if own_column:
            pl.when(source != z)(step)
        else:
            step()

    groups = []
    for c in range(len(pieces)):
        groups.append((c, True))
        if pieces[c][2]:
            groups.append((c, False))

    def take(zi, which):
        group(zi, *groups[which], True, lambda copy: copy.start())

    def take_rest(zi):
        for c in range(len(pieces)):
            if not pieces[c][2]:
                @pl.loop(0, 2)
                def _(slot):
                    arrived(slot, zi * ny + 1 - y, c)

    def hold(zi, column, mine):
        for slot in range(2):
            copy = pltpu.make_async_copy(gbuf.at[slot, zi * ny + column], held.at[slot], held_sems.at[slot])
            if slot == 0 and mine is not None:
                pl.when(jnp.logical_not(mine))(lambda copy=copy: copy.start())
            else:
                copy.start()
        for slot in range(2):
            copy = pltpu.make_async_copy(gbuf.at[slot, zi * ny + column], held.at[slot], held_sems.at[slot])
            if slot == 0 and mine is not None:
                pl.when(jnp.logical_not(mine))(lambda copy=copy: copy.wait())
            else:
                copy.wait()

    tiles = x_ref.shape[0] // tile
    width = min(256, rows)

    def rows_of(i):
        return pl.ds(pl.multiple_of(i * tile, tile), tile)

    def tiles_in(i):
        return (
            pltpu.make_async_copy(x_ref.at[rows_of(i)], x_tiles.at[0, i % 2], tile_sems.at[i % 2]),
            pltpu.make_async_copy(xbuf.at[rows_of(i)], x_tiles.at[1, i % 2], peer_sems.at[i % 2]),
        )

    def compute(column, hooks):
        def tile_out(i):
            columns = pl.ds(pl.multiple_of(column * rows, 128), rows)
            return pltpu.make_async_copy(outs.at[i % 2], done_ref.at[rows_of(i), columns], out_sems.at[i % 2])

        for copy in tiles_in(0):
            copy.start()

        @pl.loop(0, tiles)
        def _(i):
            @pl.when(i + 1 < tiles)
            def _():
                for copy in tiles_in(i + 1):
                    copy.start()

            for when, which in hooks:
                @pl.when(i == when)
                def _():
                    take(far, which)

            @pl.when(i >= 2)
            def _():
                tile_out(i - 2).wait()

            for copy in tiles_in(i):
                copy.wait()
            for at in range(0, rows, width):
                outs[i % 2, :, at:at + width] = squares(
                    scale, tokens,
                    lambda which, start: x_tiles[which, i % 2, :, start:start + LEN],
                    lambda which, start: held[which, at:at + width, start:start + LEN],
                )
            tile_out(i).start()

        for i in range(max(0, tiles - 2), tiles):
            tile_out(i).wait()

    for which in range(len(groups)):
        take(near, which)
    mine = core == owner

    @pl.when(mine)
    def _():
        for c in range(len(pieces)):
            arrived(1, own_index, c)
        local.wait()

    hold(near, y, mine)
    x_copy.wait_recv()
    early = min(2, len(groups))
    last = tiles - 1
    compute(y, [(min(3 * (k + 1), last), k) for k in range(early)])
    take_rest(near)
    hold(near, 1 - y, None)
    compute(1 - y, [(min(1 + 2 * k, last), early + k) for k in range(len(groups) - early)])
    take_rest(far)

    for c in range(len(pieces)):
        each(own_copies(c), lambda copy: copy.wait_send())
    for zi in range(zh):
        for c, own_column in groups:
            group(zi, c, own_column, False, lambda copy: copy.wait_send())
    x_copy.wait_send()


def finish_kernel(scale, near_ref, g_ref, own_ref, peer_ref, done_ref, out_ref):
    ny, rows, tokens = g_ref.shape[2:]
    near = near_ref[0]
    width = min(256, rows)
    out_ref[:, pl.ds(pl.multiple_of(near * ny * rows, 128), ny * rows)] = done_ref[...]
    for column in range(ny):
        for at in range(0, rows, width):
            start_at = pl.multiple_of(((1 - near) * ny + column) * rows + at, 128)
            out_ref[:, pl.ds(start_at, width)] = squares(
                scale, tokens,
                lambda which, start: (peer_ref if which else own_ref)[:, start:start + LEN],
                lambda which, start: g_ref[which, 0, column, at:at + width, start:start + LEN],
            )


def overlapped(nz, rot_grads, rot_inputs, lengths, token_mask):
    ny = 2
    zh = nz // 2
    rows, tokens = rot_grads.shape
    features = rot_inputs.shape[0]
    tile = next(t for t in (512, 448, 256, 64, 8) if features % t == 0)
    scale = 1.0 / (lengths.shape[0] * lax.axis_size("dp"))
    count = len(pieces_of(rows))
    dma = pltpu.SemaphoreType.DMA
    anywhere = pl.BlockSpec(memory_space=pl.ANY)
    gathered, peer_inputs, done = pl.pallas_call(
        functools.partial(gather_squares_kernel, nz, tile, scale),
        out_shape=(
            jax.ShapeDtypeStruct((2, zh * ny, rows, tokens), jnp.bfloat16),
            jax.ShapeDtypeStruct((features, tokens), jnp.bfloat16),
            jax.ShapeDtypeStruct((features, ny * rows), jnp.float32),
        ),
        in_specs=[
            pl.BlockSpec(memory_space=pltpu.VMEM),
            pl.BlockSpec(memory_space=pltpu.VMEM),
            pl.BlockSpec(memory_space=pltpu.SMEM),
            anywhere,
        ],
        out_specs=[anywhere] * 3,
        scratch_shapes=[
            pltpu.VMEM((rows, tokens), jnp.bfloat16),
            pltpu.VMEM((2, rows, tokens), jnp.bfloat16),
            pltpu.VMEM((2, 2, tile, tokens), jnp.bfloat16),
            pltpu.VMEM((2, tile, rows), jnp.float32),
            dma((count, 4)),
            dma((2, zh * ny, count, 3)),
            dma((2, zh * ny, count)),
            dma,
            dma((2,)),
            dma((2,)),
            dma((2,)),
            dma((2,)),
            dma((2,)),
        ],
        compiler_params=pltpu.CompilerParams(
            collective_id=0, has_side_effects=True, vmem_limit_bytes=GRANT
        ),
        name="gather_squares",
    )(rot_grads, token_mask.reshape(1, tokens), lengths, rot_inputs)

    grid = lax.axis_index("grid")
    near = (grid // ny > lax.axis_index("dp") * zh).astype(jnp.int32).reshape(1)
    tile = next(t for t in (TAIL_TILE, 448, 256, 64, 8) if features % t == 0)
    return pl.pallas_call(
        functools.partial(finish_kernel, scale),
        out_shape=jax.ShapeDtypeStruct((features, zh * ny * rows), jnp.float32),
        grid_spec=pltpu.PrefetchScalarGridSpec(
            num_scalar_prefetch=1,
            grid=(features // tile,),
            in_specs=[
                pl.BlockSpec(
                    (2, 1, ny, rows, tokens), lambda i, at: (0, 1 - at[0], 0, 0, 0), pipeline_mode=pl.Buffered(1)
                ),
                pl.BlockSpec((tile, tokens), lambda i, at: (i, 0)),
                pl.BlockSpec((tile, tokens), lambda i, at: (i, 0)),
                pl.BlockSpec((tile, ny * rows), lambda i, at: (i, 0)),
            ],
            out_specs=pl.BlockSpec((tile, zh * ny * rows), lambda i, at: (i, 0)),
        ),
        compiler_params=pltpu.CompilerParams(vmem_limit_bytes=GRANT),
        name="finish",
    )(near, gathered.reshape(2, zh, ny, rows, tokens), rot_inputs, peer_inputs, done)


def per_device(rot_grads, rot_inputs, lengths, token_mask):
    nz, ny = grid_sides(lax.axis_size("grid"))
    rows, tokens = rot_grads.shape
    features = rot_inputs.shape[0]
    if ny == 2 and nz == 4 and rows % 128 == 0:
        return overlapped(nz, rot_grads, rot_inputs, lengths, token_mask)
    half = nz * ny // 2
    chunks = CHUNKS if rows % (CHUNKS * 128) == 0 else 1
    slot_ids = jnp.arange(LEN, dtype=jnp.int32)
    inside = (slot_ids[None, :] < lengths[:, None]).astype(jnp.int32).reshape(-1)
    usable = token_mask * inside
    weighted = rot_grads * usable.astype(jnp.bfloat16)[None, :]

    dma = pltpu.SemaphoreType.DMA
    gathered, peer_inputs = pl.pallas_call(
        functools.partial(gather_kernel, nz, ny, chunks),
        out_shape=(
            jax.ShapeDtypeStruct((2, half, rows, tokens), jnp.bfloat16),
            jax.ShapeDtypeStruct((features, tokens), jnp.bfloat16),
        ),
        in_specs=[pl.BlockSpec(memory_space=pl.ANY)] * 2,
        out_specs=[pl.BlockSpec(memory_space=pl.ANY)] * 2,
        scratch_shapes=[
            dma((chunks, 5)),
            dma((2, half, chunks, 3)),
            dma((2, half, chunks)),
            dma,
            dma((2,)),
        ],
        compiler_params=pltpu.CompilerParams(collective_id=0, has_side_effects=True),
        name="gather",
    )(weighted, rot_inputs)

    columns = half * rows
    gathered = gathered.reshape(2, columns, tokens)
    tile = next(t for t in (512, 448, 256, 64, 8) if features % t == 0)
    spans = lengths.shape[0] * lax.axis_size("dp")
    return pl.pallas_call(
        functools.partial(square_kernel, 1.0 / spans),
        grid=(features // tile,),
        out_shape=jax.ShapeDtypeStruct((features, columns), jnp.float32),
        in_specs=[
            pl.BlockSpec((2, columns, tokens), lambda i: (0, 0, 0), pipeline_mode=pl.Buffered(1)),
            pl.BlockSpec((tile, tokens), lambda i: (i, 0)),
            pl.BlockSpec((tile, tokens), lambda i: (i, 0)),
        ],
        out_specs=pl.BlockSpec((tile, columns), lambda i: (i, 0)),
        compiler_params=pltpu.CompilerParams(vmem_limit_bytes=48 * 2**20),
        name="squares",
    )(gathered, rot_inputs, peer_inputs)


def solution(mesh):
    return jax.shard_map(
        per_device,
        mesh=mesh,
        in_specs=(
            P("grid", ("groups", "dp")),
            P("grid", ("groups", "dp")),
            P(("groups", "dp")),
            P(("groups", "dp")),
        ),
        out_specs=P(("groups", "grid"), "dp"),
        check_vma=False,
    )
```
